256 devices in a mesh: row: 32 (over y_lo, z, core), col: 8 (over y_hi, x).
Axes of the slice: x: 4, y: 4 (y_hi: 2, y_lo: 2; y = y_hi * 2 + y_lo), z: 8, core: 2. Of those that a mesh axis runs over, the one named last changes fastest.
Arguments:
- features: bfloat16 [262144, 256], P(('row', 'col')), may hold values from -6 to 6
- tile_values: bfloat16 [32, 8, 256, 128, 128], P('row', 'col'), may hold values from -0.09375 to 0.09375
- tile_rows: int32 [32, 8, 256], P('row', 'col'), may hold values from 0 to 63
- tile_cols: int32 [32, 8, 256], P('row', 'col'), may hold values from 0 to 255
- tile_count: int32 [32, 8], P('row', 'col'), may hold values from 64 to 256, as said below
- weight: bfloat16 [256, 256], replicated, may hold values from -0.375 to 0.375
Outputs:
- layer_out: bfloat16 [262144, 256], P(('row', 'col'))
The draws below stay inside these ranges and needn't reach their ends.
Inputs may be any that keep to these rules, and one draw needn't show every extreme that they name: `tile_count`: live slots of one row block and column group; some block is full in every draw.
All inputs are finite; a program needn't handle non-finite values.
Results may differ from the reference program's by a relative error of at most 0.015.
Values may be sent and summed in bfloat16 or wider, within the bound.
A program may use at most 128 MiB of HBM per device.

```python
import jax
import jax.numpy as jnp
from jax import lax

F = 256
TS = 128
NS = 1024
TILES = 256
NODES = 262144
RB = 64
CB = 256
N_ROW = 32
N_COL = 8


def draw_tile_count(key, part):
    first, second = jax.random.split(key)
    counts = jax.random.randint(first, (N_ROW * N_COL,), TILES // 4, TILES + 1)
    chosen = jax.random.randint(second, (), 0, N_ROW * N_COL)
    counts = jnp.where(jnp.arange(N_ROW * N_COL) == chosen, TILES, counts)
    return counts.reshape(N_ROW, N_COL).astype(jnp.int32)


def plant(entries, stream_key, least, top_value):
    longest = entries.shape.index(max(entries.shape))
    spots = []
    for shift in (0, 1):
        where = [jax.random.randint(jax.random.fold_in(stream_key, axis), (), 0, length) for axis, length in enumerate(entries.shape)]
        where[longest] = (where[longest] + shift) % entries.shape[longest]
        spots.append(tuple(where))
    return entries.at[spots[0]].set(least).at[spots[1]].set(top_value)


def steps_of(rng, dims, cuts, least, top_value):
    loudness, own = 1.0, jax.random.fold_in(rng, 6)
    for position, shards_of in cuts:
        steps = jnp.exp(jax.random.uniform(jax.random.fold_in(own, position), (shards_of,), jnp.float32, least / len(cuts), top_value / len(cuts)))
        loudness = loudness * jnp.repeat(steps, dims[position] // shards_of).reshape([-1 if axis == position else 1 for axis in range(len(dims))])
    return loudness


def noise(key, extent, width, most, cuts=(), kind=jnp.bfloat16):
    array = jax.random.normal(key, extent, jnp.float32) * width
    if len(cuts) > 0:
        array = steps_of(key, extent, cuts, -0.22, 0.18) * array
    return jnp.clip(array, min=-most, max=most).astype(kind)


def setup_inputs(seed: int = 0) -> dict:
    splits = jax.random.split(jax.random.key(seed), 7)
    features = noise(splits[0], (NODES, F), 1.0, 6.0, ((0, 256),))
    tile_values = noise(splits[1], (N_ROW, N_COL, TILES, TS, TS), (TS * TILES * N_COL // RB) ** -0.5, 0.09375, ((0, 32), (1, 8)))
    tile_rows = plant(jax.random.randint(splits[2], (N_ROW, N_COL, TILES), 0, RB), jax.random.fold_in(splits[2], 1), 0, RB - 1).astype(jnp.int32)
    tile_cols = plant(jax.random.randint(splits[3], (N_ROW, N_COL, TILES), 0, CB), jax.random.fold_in(splits[3], 1), 0, CB - 1).astype(jnp.int32)
    tile_count = draw_tile_count(jax.random.fold_in(splits[6], 71), 0)
    weight = noise(splits[5], (F, F), F ** -0.5, 0.375)
    return {"features": features, "tile_values": tile_values, "tile_rows": tile_rows, "tile_cols": tile_cols, "tile_count": tile_count, "weight": weight}


def block_term(slabs, values, rows_idx, cols_idx, count, c):
    group = jnp.take(slabs, c, axis=1).reshape(N_ROW * NS // TS, TS, F)
    inputs = jnp.take(group, cols_idx, axis=0).astype(jnp.float32)
    products = jnp.einsum("kij,kjf->kif", values.astype(jnp.float32), inputs)
    live = (jnp.arange(TILES) < count).astype(jnp.float32)
    products = products * live[:, None, None]
    carry = jnp.zeros((RB, TS, F), jnp.float32).at[rows_idx].add(products)
    return carry.reshape(RB * TS, F).astype(jnp.bfloat16)


def reference(features, tile_values, tile_rows, tile_cols, tile_count, weight):
    slabs = features.reshape(N_ROW, N_COL, NS, F)

    def one_row(r):
        def one_col(c):
            return block_term(slabs, tile_values[r, c], tile_rows[r, c], tile_cols[r, c], tile_count[r, c], c)
        parts = lax.map(one_col, jnp.arange(N_COL, dtype=jnp.int32))
        return jnp.sum(parts.astype(jnp.float32), axis=0)

    summed = lax.map(one_row, jnp.arange(N_ROW, dtype=jnp.int32))
    aggregated = summed.reshape(NODES, F).astype(jnp.bfloat16)
    return jnp.dot(aggregated, weight, preferred_element_type=jnp.float32).astype(jnp.bfloat16)
```

```python
import jax
import jax.numpy as jnp
from jax import lax
from jax.experimental import pallas as pl
from jax.experimental.pallas import tpu as pltpu
from jax.sharding import PartitionSpec as P

UNROLL = 4
DEPTH = 4


def tile_sums(rows, cols, count, a_hbm, x_hbm, out, acc, a_buf, x_buf, a_sem, x_sem):
    row_tiles = out.shape[0]
    n = count[0]
    groups = (n + UNROLL - 1) // UNROLL

    def copies(g, slot):
        start = pl.multiple_of(g * UNROLL, UNROLL)
        yield pltpu.make_async_copy(a_hbm.at[pl.ds(start, UNROLL)], a_buf.at[slot], a_sem.at[slot])
        for j in range(UNROLL):
            yield pltpu.make_async_copy(x_hbm.at[cols[start + j]], x_buf.at[slot, j], x_sem.at[slot, j])

    def fetch(g, slot):
        for copy in copies(g, slot):
            copy.start()

    for d in range(DEPTH - 1):
        @pl.when(d < groups)
        def _():
            fetch(d, d)

    @pl.loop(0, row_tiles)
    def _(i):
        acc[i] = jnp.zeros(acc.shape[1:], acc.dtype)

    @pl.loop(0, groups)
    def _(g):
        slot = lax.rem(g, DEPTH)
        for copy in copies(g, slot):
            copy.wait()

        @pl.when(g + DEPTH - 1 < groups)
        def _():
            fetch(g + DEPTH - 1, lax.rem(g + DEPTH - 1, DEPTH))

        for j in range(UNROLL):
            k = g * UNROLL + j
            row = jnp.where(k < n, rows[k], row_tiles)
            acc[row] += jnp.dot(a_buf[slot, j], x_buf[slot, j], preferred_element_type=jnp.float32)

    @pl.loop(0, row_tiles)
    def _(i):
        out[i] = acc[i].astype(out.dtype)


def local_sums(rows, cols, count, values, group, row_tiles):
    side, width = group.shape[1:]
    smem = pl.BlockSpec(memory_space=pltpu.SMEM)
    hbm = pl.BlockSpec(memory_space=pl.ANY)
    return pl.pallas_call(
        tile_sums,
        out_shape=jax.ShapeDtypeStruct((row_tiles, side, width), jnp.bfloat16),
        in_specs=[smem, smem, smem, hbm, hbm],
        out_specs=pl.BlockSpec(memory_space=pltpu.VMEM),
        scratch_shapes=[
            pltpu.VMEM((row_tiles + 1, side, width), jnp.float32),
            pltpu.VMEM((DEPTH, UNROLL, side, side), jnp.bfloat16),
            pltpu.VMEM((DEPTH, UNROLL, side, width), jnp.bfloat16),
            pltpu.SemaphoreType.DMA((DEPTH,)),
            pltpu.SemaphoreType.DMA((DEPTH, UNROLL)),
        ],
        name="tile_sums",
    )(rows, cols, count, values, group)


def local(features, tile_values, tile_rows, tile_cols, tile_count, weight):
    slab_rows, width = features.shape
    tiles, side = tile_values.shape[2:4]
    values = tile_values.reshape(tiles, side, side)
    row_tiles = lax.axis_size("col") * slab_rows // side
    group = lax.all_gather(features, "row", axis=0, tiled=True).reshape(-1, side, width)
    partial = local_sums(
        tile_rows.reshape(tiles), tile_cols.reshape(tiles), tile_count.reshape(1), values, group, row_tiles
    )
    summed = lax.psum_scatter(partial.reshape(row_tiles * side, width), "col", scatter_dimension=0, tiled=True)
    return jnp.dot(summed, weight, preferred_element_type=jnp.float32).astype(jnp.bfloat16)


def solution(mesh):
    return jax.shard_map(
        local,
        mesh=mesh,
        in_specs=(
            P(("row", "col"), None),
            P("row", "col", None, None, None),
            P("row", "col", None),
            P("row", "col", None),
            P("row", "col"),
            P(),
        ),
        out_specs=P(("row", "col"), None),
        check_vma=False,
    )
```

```python
import jax
import jax.numpy as jnp
from jax import lax
from jax.experimental import pallas as pl
from jax.experimental.pallas import tpu as pltpu
from jax.sharding import PartitionSpec as P

MESH = pl.DeviceIdType.MESH
SLAB = 8
RING = 8


def enter(devices):
    barrier = pltpu.get_barrier_semaphore()
    for device in devices:
        pl.semaphore_signal(barrier, inc=1, device_id=device, device_id_type=MESH)
    pl.semaphore_wait(barrier, len(devices))


class Messages:
    def __init__(self, send_sem, recv_sem):
        self.send_sem, self.recv_sem = send_sem, recv_sem
        self.index, self.sent = {}, []

    def slot(self, key):
        return self.index.setdefault(key, len(self.index))

    def copy(self, key, src, dst, device):
        slot = self.slot(key)
        return pltpu.make_async_remote_copy(
            src_ref=src, dst_ref=dst, send_sem=self.send_sem.at[slot], recv_sem=self.recv_sem.at[slot],
            device_id=device, device_id_type=MESH,
        )

    def send(self, key, src, dst, device):
        copy = self.copy(key, src, dst, device)
        copy.start()
        self.sent.append(copy)

    def arrive(self, key, dst, device):
        self.copy(key, dst, dst, device).wait_recv()

    def drain(self):
        for copy in self.sent:
            copy.wait_send()


GATHER_MESSAGES = 91


def gather_kernel(own_ref, group, send_sem, recv_sem, local_sem):
    row = lax.axis_index("row")
    half, z, core = row // 16, lax.rem(row // 2, RING), lax.rem(row, 2)

    def position(h, depth, c):
        return h * 16 + lax.rem(depth + 2 * RING, RING) * 2 + c

    up = {"row": position(half, z + 1, core)}
    down = {"row": position(half, z - 1, core)}
    side = {"row": position(1 - half, z, core)}
    twin = {"row": position(half, z, 1 - core)}
    enter((up, down, side, twin))
    messages = Messages(send_sem, recv_sem)

    def at(h, depth, c, start, size):
        return group.at[pl.ds(position(h, depth, c) * SLAB + start, size)]

    keep = pltpu.make_async_copy(own_ref, at(half, z, core, 0, SLAB), local_sem)
    keep.start()
    low, high = (0, 4), (4, 4)
    shared, shared_low, shared_high = (2, 4), (2, 2), (4, 2)
    rest_low, rest_high = (0, 2), (6, 2)

    def from_own(piece):
        return own_ref.at[pl.ds(piece[0], piece[1])]

    def ring_send(way, step, mine, piece):
        origin = z - way * (step - 1)
        owner = half if mine else 1 - half
        dst = at(owner, origin, core, *piece)
        src = from_own(piece) if mine and step == 1 else dst
        messages.send(("ring", way, step, mine, piece), src, dst, up if way > 0 else down)

    def twin_send(key, src, dst):
        messages.send(("twin",) + key, src, dst, twin)

    waiting_twin = []

    def ring_arrive(way, step, mine, piece, last):
        origin = z - way * step
        owner = half if mine else 1 - half
        here = at(owner, origin, core, *piece)
        key = ("ring", way, step, mine, piece)
        messages.arrive(key, here, up)
        if step < last:
            ring_send(way, step + 1, mine, piece)
        if mine:
            rest = rest_low if piece == low else rest_high
            part = at(half, origin, core, *rest)
            messages.send(("side", way, step, rest), part, part, side)
        twin_send(key, here, here)
        waiting_twin.append((key, at(owner, origin, 1 - core, *piece)))

    def side_arrive(key, origin, piece):
        here = at(1 - half, origin, core, *piece)
        messages.arrive(key, here, side)
        twin_send(key, here, here)
        waiting_twin.append((key, at(1 - half, origin, 1 - core, *piece)))

    ring_send(1, 1, True, low)
    ring_send(-1, 1, True, high)
    messages.send(("side", 0, 0, shared), from_own(shared), at(half, z, core, *shared), side)
    ring_send(1, 1, True, high)
    ring_send(-1, 1, True, low)
    for piece in (rest_low, rest_high):
        messages.send(("side", 0, 0, piece), from_own(piece), at(half, z, core, *piece), side)
    twin_send(("own",), own_ref, at(half, z, core, 0, SLAB))
    waiting_twin.append((("own",), at(half, z, 1 - core, 0, SLAB)))

    for step in range(1, 5):
        ring_arrive(1, step, True, low, 4)
        ring_arrive(-1, step, True, high, 4)
        if step == 1:
            side_arrive(("side", 0, 0, shared), z, shared)
            ring_send(1, 1, False, shared_low)
            ring_send(-1, 1, False, shared_high)
            ring_send(1, 1, False, shared_high)
            ring_send(-1, 1, False, shared_low)
        if step < 4:
            ring_arrive(1, step, True, high, 3)
            ring_arrive(-1, step, True, low, 3)
        if step == 1:
            side_arrive(("side", 0, 0, rest_low), z, rest_low)
            side_arrive(("side", 0, 0, rest_high), z, rest_high)
        ring_arrive(1, step, False, shared_low, 4)
        ring_arrive(-1, step, False, shared_high, 4)
        if step < 4:
            ring_arrive(1, step, False, shared_high, 3)
            ring_arrive(-1, step, False, shared_low, 3)
        side_arrive(("side", 1, step, rest_low), z - step, rest_low)
        side_arrive(("side", -1, step, rest_high), z + step, rest_high)
        if step < 4:
            side_arrive(("side", 1, step, rest_high), z - step, rest_high)
            side_arrive(("side", -1, step, rest_low), z + step, rest_low)
    for key, here in waiting_twin:
        messages.arrive(("twin",) + key, here, twin)
    keep.wait()
    messages.drain()
    assert len(messages.index) == GATHER_MESSAGES, len(messages.index)


def gather_group(own):
    n, side, width = own.shape
    return pl.pallas_call(
        gather_kernel,
        out_shape=jax.ShapeDtypeStruct((4 * RING * n, side, width), own.dtype),
        in_specs=[pl.BlockSpec(memory_space=pltpu.VMEM)],
        out_specs=pl.BlockSpec(memory_space=pl.ANY),
        scratch_shapes=[
            pltpu.SemaphoreType.DMA((GATHER_MESSAGES,)),
            pltpu.SemaphoreType.DMA((GATHER_MESSAGES,)),
            pltpu.SemaphoreType.DMA,
        ],
        compiler_params=pltpu.CompilerParams(collective_id=0, has_side_effects=True),
        name="gather_group",
    )(own)


SCATTER_MESSAGES = 20


def scatter_kernel(part, out, x_in, turn, total, y_in, relay, send_sem, recv_sem):
    row, col = lax.axis_index("row"), lax.axis_index("col")
    y_lo, y_hi, x = row // 16, col // 4, lax.rem(col, 4)

    def x_peer(way):
        return {"col": y_hi * 4 + lax.rem(x + way + 4, 4)}

    def y_peer(way):
        y = lax.rem(y_hi * 2 + y_lo + way + 4, 4)
        return {"row": lax.rem(row, 16) + lax.rem(y, 2) * 16, "col": (y // 2) * 4 + x}

    peers = {("x", 1): x_peer(1), ("x", -1): x_peer(-1), ("y", 1): y_peer(1), ("y", -1): y_peer(-1)}
    enter(tuple(peers.values()))
    messages = Messages(send_sem, recv_sem)
    both = (1, -1)

    def chunk(far, way, start):
        band = 1 - y_hi if far else y_hi
        return pl.ds((band * 4 + lax.rem(x + way + 4, 4)) * SLAB + start, 4)

    def x_send(kind, far, way, src):
        messages.send(("x", kind, far, way), src, x_in.at[kind, far, (way + 1) // 2], peers["x", way])

    def x_arrive(kind, far, way):
        here = x_in.at[kind, far, (way + 1) // 2]
        messages.arrive(("x", kind, far, way), here, peers["x", way])
        return here

    def through(way):
        return 0 if way > 0 else 4

    def first(far):
        for way in both:
            x_send(0, far, way, part.at[chunk(far, 2 * way, through(way))])
        for way in both:
            x_send(1, far, way, part.at[chunk(far, way, through(-way))])

    def second(far):
        for way in both:
            here = x_arrive(0, far, way)
            base = chunk(far, way, through(way)).start
            for t in range(4):
                turn[far, (way + 1) // 2, t] = (
                    part[base + t].astype(jnp.float32) + here[t].astype(jnp.float32)
                ).astype(turn.dtype)
            x_send(2, far, way, turn.at[far, (way + 1) // 2])

    def last(far, extra, store):
        for way in both:
            one = x_arrive(1, far, -way)
            two = x_arrive(2, far, way)
            more = extra(way)
            base = chunk(far, 0, through(way)).start
            for t in range(4):
                value = part[base + t].astype(jnp.float32) + one[t].astype(jnp.float32) + two[t].astype(jnp.float32)
                if more is not None:
                    value = value + more[t].astype(jnp.float32)
                store(way, t, value)
            if far:
                messages.send(("y", 0, way), total.at[(way + 1) // 2], relay.at[(way + 1) // 2], peers["y", way])

    first(1)
    second(1)
    first(0)

    def store_total(way, t, value):
        total[(way + 1) // 2, t] = value.astype(total.dtype)

    last(1, lambda way: None, store_total)
    second(0)
    for way in both:
        here = relay.at[(way + 1) // 2]
        messages.arrive(("y", 0, way), here, peers["y", way])
        messages.send(("y", 1, way), here, y_in.at[(way + 1) // 2], peers["y", way])

    def final(way):
        here = y_in.at[(way + 1) // 2]
        messages.arrive(("y", 1, way), here, peers["y", way])
        return here

    def store_out(way, t, value):
        out[through(way) + t] = value.astype(out.dtype)

    last(0, final, store_out)
    messages.drain()


def scatter_sums(part):
    n, side, width = part.shape
    piece = (4, side, width)
    vmem = pl.BlockSpec(memory_space=pltpu.VMEM)
    return pl.pallas_call(
        scatter_kernel,
        out_shape=jax.ShapeDtypeStruct((SLAB, side, width), part.dtype),
        in_specs=[vmem],
        out_specs=vmem,
        scratch_shapes=[
            pltpu.VMEM((3, 2, 2) + piece, part.dtype),
            pltpu.VMEM((2, 2) + piece, part.dtype),
            pltpu.VMEM((2,) + piece, part.dtype),
            pltpu.VMEM((2,) + piece, part.dtype),
            pltpu.VMEM((2,) + piece, part.dtype),
            pltpu.SemaphoreType.DMA((SCATTER_MESSAGES,)),
            pltpu.SemaphoreType.DMA((SCATTER_MESSAGES,)),
        ],
        compiler_params=pltpu.CompilerParams(collective_id=1, has_side_effects=True),
        name="scatter_sums",
    )(part)


UNROLL = 4
DEPTH = 4


def tile_sums(rows, cols, count, a_hbm, x_hbm, out, acc, a_buf, x_buf, a_sem, x_sem):
    row_tiles = out.shape[0]
    n = count[0]
    groups = (n + UNROLL - 1) // UNROLL

    def copies(g, slot):
        start = pl.multiple_of(g * UNROLL, UNROLL)
        yield pltpu.make_async_copy(a_hbm.at[pl.ds(start, UNROLL)], a_buf.at[slot], a_sem.at[slot])
        for j in range(UNROLL):
            yield pltpu.make_async_copy(x_hbm.at[cols[start + j]], x_buf.at[slot, j], x_sem.at[slot, j])

    def fetch(g, slot):
        for copy in copies(g, slot):
            copy.start()

    for d in range(DEPTH - 1):
        @pl.when(d < groups)
        def _():
            fetch(d, d)

    @pl.loop(0, row_tiles)
    def _(i):
        acc[i] = jnp.zeros(acc.shape[1:], acc.dtype)

    @pl.loop(0, groups)
    def _(g):
        slot = lax.rem(g, DEPTH)
        for copy in copies(g, slot):
            copy.wait()

        @pl.when(g + DEPTH - 1 < groups)
        def _():
            fetch(g + DEPTH - 1, lax.rem(g + DEPTH - 1, DEPTH))

        for j in range(UNROLL):
            k = g * UNROLL + j
            row = jnp.where(k < n, rows[k], row_tiles)
            acc[row] += jnp.dot(a_buf[slot, j], x_buf[slot, j], preferred_element_type=jnp.float32)

    @pl.loop(0, row_tiles)
    def _(i):
        out[i] = acc[i].astype(out.dtype)


def local_sums(rows, cols, count, values, group, row_tiles):
    side, width = group.shape[1:]
    smem = pl.BlockSpec(memory_space=pltpu.SMEM)
    hbm = pl.BlockSpec(memory_space=pl.ANY)
    return pl.pallas_call(
        tile_sums,
        out_shape=jax.ShapeDtypeStruct((row_tiles, side, width), jnp.bfloat16),
        in_specs=[smem, smem, smem, hbm, hbm],
        out_specs=pl.BlockSpec(memory_space=pltpu.VMEM),
        scratch_shapes=[
            pltpu.VMEM((row_tiles + 1, side, width), jnp.float32),
            pltpu.VMEM((DEPTH, UNROLL, side, side), jnp.bfloat16),
            pltpu.VMEM((DEPTH, UNROLL, side, width), jnp.bfloat16),
            pltpu.SemaphoreType.DMA((DEPTH,)),
            pltpu.SemaphoreType.DMA((DEPTH, UNROLL)),
        ],
        name="tile_sums",
    )(rows, cols, count, values, group)


def local(features, tile_values, tile_rows, tile_cols, tile_count, weight):
    slab_rows, width = features.shape
    tiles, side = tile_values.shape[2:4]
    values = tile_values.reshape(tiles, side, side)
    row_tiles = lax.axis_size("col") * slab_rows // side
    group = gather_group(features.reshape(slab_rows // side, side, width))
    partial = local_sums(
        tile_rows.reshape(tiles), tile_cols.reshape(tiles), tile_count.reshape(1), values, group, row_tiles
    )
    summed = scatter_sums(partial).reshape(slab_rows, width)
    return jnp.dot(summed, weight, preferred_element_type=jnp.float32).astype(jnp.bfloat16)


def solution(mesh):
    return jax.shard_map(
        local,
        mesh=mesh,
        in_specs=(
            P(("row", "col"), None),
            P("row", "col", None, None, None),
            P("row", "col", None),
            P("row", "col", None),
            P("row", "col"),
            P(),
        ),
        out_specs=P(("row", "col"), None),
        check_vma=False,
    )
```

```python
import jax
import jax.numpy as jnp
from jax import lax
from jax.experimental import pallas as pl
from jax.experimental.pallas import tpu as pltpu
from jax.sharding import PartitionSpec as P

MESH = pl.DeviceIdType.MESH
SLAB = 8
RING = 8
HALF = 128
STEPS = 8
PIECES = 8
GATHER_COPIES = 91
SCATTER_COPIES = 16
COPIES = GATHER_COPIES + SCATTER_COPIES


def plan_kernel(count, rows, cols, out):
    n = rows.shape[1]
    rows_in_all = 64
    f32 = jnp.float32
    lane = lax.broadcasted_iota(jnp.int32, (n, n), 1).astype(f32)
    sub = lax.broadcasted_iota(jnp.int32, (n, n), 0).astype(f32)
    spot = lax.broadcasted_iota(jnp.int32, (1, n), 1)
    row = jnp.where(spot < count[0], rows[...], rows_in_all).astype(f32)
    key = row * n + spot.astype(f32)

    def turned(line):
        return jnp.sum(jnp.where(lane == sub, line, 0.0), axis=1, keepdims=True)

    row_t, key_t, col_t = turned(row), turned(key), turned(cols[...].astype(f32))
    rank_t = jnp.sum(jnp.where(key < key_t, 1.0, 0.0), axis=1, keepdims=True)
    hit = rank_t == lane

    def placed(line):
        return jnp.sum(jnp.where(hit, line, 0.0), axis=0, keepdims=True)

    row_s = placed(row_t)
    keep = jnp.where((row_s == pltpu.roll(row_s, 1, 1)) & (spot > 0), 1.0, 0.0)
    upto = jnp.sum(jnp.where(row_t <= lane, 1.0, 0.0), axis=0, keepdims=True)
    below = jnp.sum(jnp.where(row_t < lane, 1.0, 0.0), axis=0, keepdims=True)
    lines = (placed(sub), placed(col_t), keep, jnp.maximum(upto - 1.0, 0.0), jnp.where(upto > below, 1.0, 0.0))
    for i, line in enumerate(lines):
        out[i : i + 1] = line.astype(jnp.int32)


def plan(count, rows, cols):
    vmem = pl.BlockSpec(memory_space=pltpu.VMEM)
    return pl.pallas_call(
        plan_kernel,
        out_shape=jax.ShapeDtypeStruct((8, rows.shape[1]), jnp.int32),
        in_specs=[pl.BlockSpec(memory_space=pltpu.SMEM), vmem, vmem],
        out_specs=vmem,
        name="plan",
    )(count, rows, cols)


def enter(devices):
    barrier = pltpu.get_barrier_semaphore()
    for device in devices:
        pl.semaphore_signal(barrier, inc=1, device_id=device, device_id_type=MESH)
    pl.semaphore_wait(barrier, len(devices))


class Messages:
    def __init__(self, send_sem, recv_sem):
        self.send_sem, self.recv_sem = send_sem, recv_sem
        self.index, self.sent = {}, []

    def copy(self, key, src, dst, device):
        slot = self.index.setdefault(key, len(self.index))
        return pltpu.make_async_remote_copy(
            src_ref=src, dst_ref=dst, send_sem=self.send_sem.at[slot], recv_sem=self.recv_sem.at[slot],
            device_id=device, device_id_type=MESH,
        )

    def send(self, key, src, dst, device):
        copy = self.copy(key, src, dst, device)
        copy.start()
        self.sent.append(copy)

    def arrive(self, key, dst, device):
        self.copy(key, dst, dst, device).wait_recv()

    def drain(self):
        for copy in self.sent:
            copy.wait_send()


def gather(messages, peers, place, own, group):
    half, z, core = place
    up, down, side, twin = peers

    def at(h, depth, c, start, size):
        position = h * 16 + lax.rem(depth + 2 * RING, RING) * 2 + c
        return group.at[pl.ds(position * SLAB + start, size)]

    low, high = (0, 4), (4, 4)
    shared, shared_low, shared_high = (2, 4), (2, 2), (4, 2)
    rest_low, rest_high = (0, 2), (6, 2)
    waiting = []

    def ring_send(way, step, mine, piece):
        dst = at(half if mine else 1 - half, z - way * (step - 1), core, *piece)
        src = own(*piece) if mine and step == 1 else dst
        messages.send(("ring", way, step, mine, piece), src, dst, up if way > 0 else down)

    def to_twin(key, here, owner, origin, piece):
        messages.send(("twin",) + key, here, here, twin)
        waiting.append((("twin",) + key, at(owner, origin, 1 - core, *piece)))

    def ring_arrive(way, step, mine, piece, last):
        origin, owner = z - way * step, half if mine else 1 - half
        here, key = at(owner, origin, core, *piece), ("ring", way, step, mine, piece)
        messages.arrive(key, here, up)
        if step < last:
            ring_send(way, step + 1, mine, piece)
        if mine:
            rest = rest_low if piece == low else rest_high
            part = at(half, origin, core, *rest)
            messages.send(("side", way, step, rest), part, part, side)
        to_twin(key, here, owner, origin, piece)

    def side_arrive(key, origin, piece):
        here = at(1 - half, origin, core, *piece)
        messages.arrive(key, here, side)
        to_twin(key, here, 1 - half, origin, piece)

    ring_send(1, 1, True, low)
    ring_send(-1, 1, True, high)
    messages.send(("side", 0, 0, shared), own(*shared), at(half, z, core, *shared), side)
    ring_send(1, 1, True, high)
    ring_send(-1, 1, True, low)
    for piece in (rest_low, rest_high):
        messages.send(("side", 0, 0, piece), own(*piece), at(half, z, core, *piece), side)
    messages.send(("twin", "own"), own(0, SLAB), at(half, z, core, 0, SLAB), twin)
    waiting.append((("twin", "own"), at(half, z, 1 - core, 0, SLAB)))
    yield 0

    for step in range(1, 5):
        ring_arrive(1, step, True, low, 4)
        yield step
        ring_arrive(-1, step, True, high, 4)
        yield step
        if step == 1:
            side_arrive(("side", 0, 0, shared), z, shared)
            for way, piece in ((1, shared_low), (-1, shared_high), (1, shared_high), (-1, shared_low)):
                ring_send(way, 1, False, piece)
            yield step
        if step < 4:
            ring_arrive(1, step, True, high, 3)
            yield step
            ring_arrive(-1, step, True, low, 3)
            yield step
        if step == 1:
            side_arrive(("side", 0, 0, rest_low), z, rest_low)
            side_arrive(("side", 0, 0, rest_high), z, rest_high)
            yield step
        ring_arrive(1, step, False, shared_low, 4)
        yield step
        ring_arrive(-1, step, False, shared_high, 4)
        yield step
        if step < 4:
            ring_arrive(1, step, False, shared_high, 3)
            yield step
            ring_arrive(-1, step, False, shared_low, 3)
            yield step
        side_arrive(("side", 1, step, rest_low), z - step, rest_low)
        side_arrive(("side", -1, step, rest_high), z + step, rest_high)
        yield step
        if step < 4:
            side_arrive(("side", 1, step, rest_high), z - step, rest_high)
            side_arrive(("side", -1, step, rest_low), z + step, rest_low)
            yield step
    for key, here in waiting:
        messages.arrive(key, here, twin)
    yield 5


def products(tables, values, group, running, sums, part):
    groups = values.shape[0] // STEPS // PIECES

    def body(g):
        total = running[...]
        for j in range(STEPS):
            s = g * STEPS + j
            product = jnp.dot(values[tables[0, s]], group[tables[1, s]], preferred_element_type=jnp.float32)
            total = product + total * tables[2, s].astype(jnp.float32)
            sums[s] = total.astype(sums.dtype)
        running[...] = total

    running[...] = jnp.zeros(running.shape, running.dtype)
    for piece in range(PIECES):
        pl.loop(piece * groups, (piece + 1) * groups)(body)
        yield

    @pl.loop(0, part.shape[0])
    def _(i):
        part[i] = sums[tables[3, i]] * tables[4, i].astype(jnp.float32).astype(sums.dtype)


def scatter(messages, peers, place, part, store_out, x_in, turn, total, relay, y_in):
    y_hi, x = place
    both = (1, -1)

    def chunk(far, way, start):
        band = 1 - y_hi if far else y_hi
        return (band * 4 + lax.rem(x + way + 4, 4)) * SLAB + start

    def x_send(kind, far, way, src):
        messages.send(("x", kind, far, way), src, x_in.at[kind, far, (way + 1) // 2], peers["x", way])

    def x_arrive(kind, far, way):
        here = x_in.at[kind, far, (way + 1) // 2]
        messages.arrive(("x", kind, far, way), here, peers["x", way])
        return here

    def through(way):
        return 0 if way > 0 else 4

    def first(far):
        for way in both:
            x_send(0, far, way, part.at[pl.ds(chunk(far, 2 * way, through(way)), 4)])
        for way in both:
            x_send(1, far, way, part.at[pl.ds(chunk(far, way, through(-way)), 4)])

    def second(far):
        for way in both:
            here, base, side = x_arrive(0, far, way), chunk(far, way, through(way)), (way + 1) // 2
            for t in range(4):
                both_parts = part[base + t].astype(jnp.float32) + here[t].astype(jnp.float32)
                turn[far, side, t] = both_parts.astype(turn.dtype)
            x_send(2, far, way, turn.at[far, side])

    def last(far, way, more, store):
        one, two, base = x_arrive(1, far, -way), x_arrive(2, far, way), chunk(far, 0, through(way))
        for t in range(4):
            value = part[base + t].astype(jnp.float32) + one[t].astype(jnp.float32) + two[t].astype(jnp.float32)
            if more is not None:
                value = value + more[t].astype(jnp.float32)
            store(t, value)

    first(1)
    yield
    second(1)
    first(0)
    yield
    for way in both:
        side = (way + 1) // 2

        def store_total(t, value):
            total[side, t] = value.astype(total.dtype)

        last(1, way, None, store_total)
        messages.send(("y", 0, way), total.at[side], relay.at[side], peers["y", way])
    yield
    second(0)
    yield
    for way in both:
        here = relay.at[(way + 1) // 2]
        messages.arrive(("y", 0, way), here, peers["y", way])
        messages.send(("y", 1, way), here, y_in.at[(way + 1) // 2], peers["y", way])
    yield
    for way in both:
        here = y_in.at[(way + 1) // 2]
        messages.arrive(("y", 1, way), here, peers["y", way])
        last(0, way, here, lambda t, value: store_out(through(way) + t, value))
    yield


def layer_kernel(tables, own, values_hbm, out, *scratch):
    values, sums = scratch[:2]
    groups, parts = scratch[2:4], scratch[4:6]
    buffers = (scratch[6:11], scratch[11:16])
    sems, values_sem, keep_sem, running = (scratch[16:18], scratch[18:20]), scratch[20], scratch[21], scratch[22]
    row, col = lax.axis_index("row"), lax.axis_index("col")
    half, z, core = row // 16, lax.rem(row // 2, RING), lax.rem(row, 2)
    y_hi, x = col // 4, lax.rem(col, 4)

    def ring_peer(h, depth, c):
        return {"row": h * 16 + lax.rem(depth + RING, RING) * 2 + c}

    def x_peer(way):
        return {"col": y_hi * 4 + lax.rem(x + way + 4, 4)}

    def y_peer(way):
        y = lax.rem(y_hi * 2 + half + way + 4, 4)
        return {"row": lax.rem(row, 16) + lax.rem(y, 2) * 16, "col": (y // 2) * 4 + x}

    ring = (ring_peer(half, z + 1, core), ring_peer(half, z - 1, core), ring_peer(1 - half, z, core), ring_peer(half, z, 1 - core))
    cross = {("x", 1): x_peer(1), ("x", -1): x_peer(-1), ("y", 1): y_peer(1), ("y", -1): y_peer(-1)}
    enter(ring + tuple(cross.values()))
    load = pltpu.make_async_copy(values_hbm, values, values_sem)

    gathers, scatters, keeps, talks = [], [], [], []
    for h in range(2):
        lanes = pl.ds(h * HALF, HALF)
        messages = Messages(*sems[h])
        talks.append(messages)

        def own_piece(start, size, lanes=lanes):
            return own.at[pl.ds(start, size), :, lanes]

        def store_out(t, value, lanes=lanes):
            out[t, :, lanes] = value.astype(out.dtype)

        gathers.append(gather(messages, ring, (half, z, core), own_piece, groups[h]))
        scatters.append(scatter(messages, cross, (y_hi, x), parts[h], store_out, *buffers[h]))
        keeps.append(pltpu.make_async_copy(own.at[:, :, lanes], groups[h].at[pl.ds(row * SLAB, SLAB)], keep_sem.at[h]))

    multiply = [products(tables, values, groups[h], running, sums, parts[h]) for h in range(2)]
    acts = {"g0": gathers[0], "g1": gathers[1], "s0": scatters[0], "s1": scatters[1], "m0": multiply[0], "m1": multiply[1]}
    next(gathers[0])
    for keep in keeps:
        keep.start()
    load.start()
    for name in ORDER:
        if name == "local":
            load.wait()
            for keep in keeps:
                keep.wait()
        else:
            next(acts[name], None)
    for gen in acts.values():
        for _ in gen:
            pass
    for messages in talks:
        messages.drain()
        assert len(messages.index) == COPIES


def spread(*lists):
    tagged = []
    for n, items in enumerate(lists):
        tagged += [((i + 0.5) / len(items), n, item) for i, item in enumerate(items)]
    return [item for _, _, item in sorted(tagged)]


ORDER = (
    ["g0"] * 32 + ["g1"] + ["g0"] * 6 + ["local"]
    + spread(["m0"] * (PIECES + 1), ["g1"] * 12) + ["s0"]
    + ["g1"] * 10 + ["s0"]
    + ["g1"] * 5 + ["s0"] + ["g1"] * 5 + ["s0"]
    + ["g1"] * 5 + ["s0"] + ["g1"]
    + ["m1"] * (PIECES + 1) + ["s1"] + ["s0"] + ["s1"] * 5
)


def layer(tables, own, values):
    slab, side, width = own.shape
    tiles = values.shape[0]
    bf16 = own.dtype
    piece = (4, side, HALF)
    vmem = pl.BlockSpec(memory_space=pltpu.VMEM)
    sums = pltpu.VMEM((tiles, side, HALF), bf16)
    group = pltpu.VMEM((4 * RING * slab, side, HALF), bf16)
    part = pltpu.VMEM((8 * slab, side, HALF), bf16)
    buffers = [
        pltpu.VMEM((3, 2, 2) + piece, bf16),
        pltpu.VMEM((2, 2) + piece, bf16),
        pltpu.VMEM((2,) + piece, bf16),
        pltpu.VMEM((2,) + piece, bf16),
        pltpu.VMEM((2,) + piece, bf16),
    ]
    sems = [pltpu.SemaphoreType.DMA((COPIES,)), pltpu.SemaphoreType.DMA((COPIES,))]
    return pl.pallas_call(
        layer_kernel,
        out_shape=jax.ShapeDtypeStruct((slab, side, width), bf16),
        in_specs=[pl.BlockSpec(memory_space=pltpu.SMEM), vmem, pl.BlockSpec(memory_space=pl.ANY)],
        out_specs=vmem,
        scratch_shapes=[pltpu.VMEM(values.shape, bf16), sums, group, group, part, part]
        + buffers + buffers + sems + sems + [pltpu.SemaphoreType.DMA, pltpu.SemaphoreType.DMA((2,)), pltpu.VMEM((side, HALF), jnp.float32)],
        compiler_params=pltpu.CompilerParams(collective_id=0, has_side_effects=True, vmem_limit_bytes=60 * 1024 * 1024),
        name="layer",
    )(tables, own, values)


def local(features, tile_values, tile_rows, tile_cols, tile_count, weight):
    slab_rows, width = features.shape
    tiles, side = tile_values.shape[2:4]
    tables = plan(tile_count.reshape(1), tile_rows.reshape(1, tiles), tile_cols.reshape(1, tiles))
    summed = layer(tables, features.reshape(-1, side, width), tile_values.reshape(tiles, side, side))
    return jnp.dot(summed.reshape(slab_rows, width), weight, preferred_element_type=jnp.float32).astype(jnp.bfloat16)


def solution(mesh):
    return jax.shard_map(
        local,
        mesh=mesh,
        in_specs=(
            P(("row", "col"), None),
            P("row", "col", None, None, None),
            P("row", "col", None),
            P("row", "col", None),
            P("row", "col"),
            P(),
        ),
        out_specs=P(("row", "col"), None),
        check_vma=False,
    )
```
